512 devices in a mesh: alpha: 64 (over y, z), beta: 8 (over x, core).
Axes of the slice: x: 4, y: 4, z: 16, core: 2. Of those that a mesh axis runs over, the one named last changes fastest.
Arguments:
- coeffs: bfloat16 [512, 2, 1024], P('alpha', None, 'beta'), may hold values from -6 to 6
- integrals: bfloat16 [484, 484], replicated, may hold values from -0.03125 to 0.03125
- beta_source: int32 [484, 1024], P(None, 'beta'), may hold values from 0 to 1023
- beta_sign: int32 [484, 1024], P(None, 'beta'), may hold values from -1 to 1
- alpha_slots: int32 [64, 64, 4, 128], P('alpha'), may hold values from -1 to 483, as said below
Outputs:
- sigma: float32 [512, 2, 1024], P('alpha', None, 'beta')
The draws below stay inside these ranges and needn't reach their ends.
Inputs may be any that keep to these rules, and one draw needn't show every extreme that they name: alpha_slots[s, d, 0, q], [s, d, 1, q], [s, d, 2, q], [s, d, 3, q] are the source string within block s (below 8), the orbital pair (below 484), the target string within block d (below 8) and the sign (-1 or 1; 0 marks an empty slot, whose other entries mean nothing); in every draw some target block has all 128 slots live from every source block.
All inputs are finite; a program needn't handle non-finite values.
Results may differ from the reference program's by a relative error of at most 0.0029.
Values may be sent and summed in bfloat16 or wider, within the bound.
No kernel may reach another device: no remote copies, remote signals or barrier semaphores. Data moves between devices by JAX's collectives and lax.ppermute only.
A program may use at most 64 MiB of HBM per device.

```python
import jax
import jax.numpy as jnp
from jax import lax

P_SIZE = 484
A_DEV = 8
CAP = 128
ABLOCKS = 64
NA = 512
NB = 1024


def draw_alpha_slots(key, part):
    shape = (ABLOCKS, ABLOCKS, CAP)
    source_ids = jax.random.randint(jax.random.fold_in(key, 11), shape, 0, A_DEV)
    pair_ids = jax.random.randint(jax.random.fold_in(key, 12), shape, 0, P_SIZE)
    target_ids = jax.random.randint(jax.random.fold_in(key, 13), shape, 0, A_DEV)
    sign_vals = jax.random.randint(jax.random.fold_in(key, 14), shape, 0, 2) * 2 - 1
    hot_rows = jax.random.randint(jax.random.fold_in(key, 15), (ABLOCKS,), 0, 2)
    forced = jax.random.randint(jax.random.fold_in(key, 16), (), 0, ABLOCKS)
    hot_rows = jnp.where(jnp.arange(ABLOCKS) == forced, 1, hot_rows)
    base_count = jax.random.randint(jax.random.fold_in(key, 17), (ABLOCKS, ABLOCKS), CAP // 4, CAP // 2 + 1)
    counts = jnp.where(hot_rows[None, :] == 1, CAP, base_count)
    mult = jax.random.randint(jax.random.fold_in(key, 18), (ABLOCKS, ABLOCKS), 0, CAP // 2) * 2 + 1
    offset = jax.random.randint(jax.random.fold_in(key, 19), (ABLOCKS, ABLOCKS), 0, CAP)
    position = (jnp.arange(CAP)[None, None, :] * mult[:, :, None] + offset[:, :, None]) % CAP
    live = position < counts[:, :, None]
    sign_vals = jnp.where(live, sign_vals, 0)
    return jnp.stack([source_ids, pair_ids, target_ids, sign_vals], axis=2).astype(jnp.int32)


def plant(entries, rng, smallest, largest):
    place = [jax.random.randint(jax.random.fold_in(rng, axis), (), 0, length) for axis, length in enumerate(entries.shape)]
    main_axis = entries.shape.index(max(entries.shape))
    next_to = place[:main_axis] + [(place[main_axis] + 1) % entries.shape[main_axis]] + place[main_axis + 1:]
    return entries.at[tuple(place)].set(smallest).at[tuple(next_to)].set(largest)


def block_scale(own_key, dims, pieces, smallest, high):
    loudness = 1.0
    for dim, blocks in pieces:
        steps = jax.random.uniform(jax.random.fold_in(jax.random.fold_in(own_key, 6), dim), (blocks,), jnp.float32, smallest / len(pieces), high / len(pieces))
        loudness = loudness * jnp.repeat(jnp.exp(steps), dims[dim] // blocks).reshape((-1,) + (1,) * (len(dims) - 1 - dim))
    return loudness


def normal_values(own_key, dims, spread, bound, cuts=(), held_as=jnp.bfloat16):
    loudness = block_scale(own_key, dims, cuts, -0.22, 0.18) if cuts else 1.0
    entries = jax.random.normal(own_key, dims, jnp.float32) * spread * loudness
    return jnp.minimum(jnp.maximum(entries, -bound), bound).astype(held_as)


def setup_inputs(seed: int = 0) -> dict:
    key_list = jax.random.split(jax.random.key(seed), 6)
    coeffs = normal_values(key_list[0], (NA, 2, NB), 1.0, 6.0, ((0, 64), (2, 8)))
    integrals = normal_values(key_list[1], (P_SIZE, P_SIZE), (64 * P_SIZE) ** -0.5, 0.03125)
    beta_source = plant(jax.random.randint(key_list[2], (P_SIZE, NB), 0, NB), jax.random.fold_in(key_list[2], 1), 0, NB - 1).astype(jnp.int32)
    beta_sign = plant(jax.random.randint(key_list[3], (P_SIZE, NB), -1, 2), jax.random.fold_in(key_list[3], 1), -1, 1).astype(jnp.int32)
    alpha_slots = draw_alpha_slots(jax.random.fold_in(key_list[5], 71), 0)
    return {"coeffs": coeffs, "integrals": integrals, "beta_source": beta_source, "beta_sign": beta_sign, "alpha_slots": alpha_slots}


def reference(coeffs, integrals, beta_source, beta_sign, alpha_slots):
    signs_beta = beta_sign.astype(jnp.float32)
    int_mat = integrals.astype(jnp.float32)
    strings = jnp.arange(A_DEV, dtype=jnp.int32)

    def one_block(carry, block_id):
        block_rows = lax.dynamic_slice_in_dim(coeffs, (block_id * A_DEV).astype(jnp.int32), A_DEV, 0).astype(jnp.float32)
        d_block = jnp.take(block_rows, beta_source, axis=2) * signs_beta
        e_block = jnp.einsum('kp,acpb->kacb', int_mat, d_block)
        e_block = lax.optimization_barrier(e_block.astype(jnp.bfloat16)).astype(jnp.float32)
        slot_table = alpha_slots[block_id]
        source_ids = slot_table[:, 0]
        pair_ids = slot_table[:, 1]
        target_ids = slot_table[:, 2]
        sign_vals = slot_table[:, 3].astype(jnp.float32)
        picked = e_block[pair_ids, source_ids] * sign_vals[:, :, None, None]
        one_hot = (target_ids[:, :, None] == strings).astype(jnp.float32)
        contrib = jnp.einsum('dqa,dqcb->dacb', one_hot, picked)
        return carry + contrib.reshape(ABLOCKS * A_DEV, 2, NB), None

    start = jnp.zeros((ABLOCKS * A_DEV, 2, NB), jnp.float32)
    sigma, unused = lax.scan(one_block, start, jnp.arange(ABLOCKS, dtype=jnp.int32))
    return sigma
```

```python
import jax
import jax.numpy as jnp
from jax import lax
from jax.experimental import pallas as pl
from jax.experimental.pallas import tpu as pltpu
from jax.sharding import Mesh
from jax.sharding import PartitionSpec as P

BF16 = jnp.bfloat16
F32 = jnp.float32


def gather_kernel(c_ref, idx_ref, sgn_ref, d_ref, c32_ref):
    blocks, rows, _ = c_ref.shape
    pairs = idx_ref.shape[0]
    for j in range(blocks):
        c32_ref[j] = c_ref[j].astype(F32)

    def do(p0, n):
        idx = idx_ref[pl.ds(p0, n), :]
        sgn = sgn_ref[pl.ds(p0, n), :].astype(F32)
        hi = lax.shift_right_logical(idx, 7)
        lo = idx & 127
        masks = [hi == j for j in range(blocks)]
        for x in range(rows):
            acc = None
            for j in range(blocks):
                t = jnp.broadcast_to(c32_ref[j, x : x + 1, :], (8, 128))
                g = [
                    jnp.take_along_axis(t[: min(8, n)], lo[r : r + 8], axis=1, mode="promise_in_bounds")
                    for r in range(0, n, 8)
                ]
                g = jnp.concatenate(g, axis=0) if n > 8 else g[0]
                acc = g if acc is None else jnp.where(masks[j], g, acc)
            d_ref[pl.ds(p0, n), x * 128 : (x + 1) * 128] = (acc * sgn).astype(BF16)

    def body(i, carry):
        do(pl.multiple_of(i * 16, 16), 16)
        return carry

    lax.fori_loop(0, pairs // 16, body, 0)
    if pairs % 16:
        do(pairs // 16 * 16, pairs % 16)


def slot_kernel(s_ref, m_ref):
    width = m_ref.shape[2]
    rows = lax.broadcasted_iota(jnp.int32, (128, 128), 0)
    krow = lax.broadcasted_iota(jnp.int32, (width, 128), 0)

    def body(i, carry):
        picks, pairs = [], []
        for e in range(2):
            d = i * 2 + e
            code = s_ref[d, 0:1, :] * 16 + e * 8 + s_ref[d, 2:3, :]
            sign = s_ref[d, 3:4, :].astype(F32)
            picks.append(jnp.where(rows == code, sign, 0.0).astype(BF16))
            pairs.append(jnp.where(krow == s_ref[d, 1:2, :], 1.0, 0.0).astype(BF16))
        m = lax.dot_general(
            jnp.concatenate(picks, axis=1),
            jnp.concatenate(pairs, axis=1),
            (((1,), (1,)), ((), ())),
            preferred_element_type=F32,
        ).astype(BF16)
        for a in range(8):
            m_ref[a, pl.ds(pl.multiple_of(i * 16, 16), 16), :] = m[a * 16 : (a + 1) * 16, :]
        return carry

    lax.fori_loop(0, s_ref.shape[0] // 2, body, 0)


def sum_kernel(v_ref, d_ref, m_ref, o_ref, e_ref):
    pairs = v_ref.shape[0]
    for h in range(4):
        e = jnp.dot(v_ref[...], d_ref[:, h * 512 : (h + 1) * 512], preferred_element_type=F32)
        e_ref[:, h * 512 : (h + 1) * 512] = e.astype(BF16)
    acc = None
    for a in range(8):
        t = jnp.dot(m_ref[a, :, 0:pairs], e_ref[:, a * 256 : (a + 1) * 256], preferred_element_type=F32)
        acc = t if acc is None else acc + t
    o_ref[...] = acc.astype(o_ref.dtype)


def local(coeffs, integrals, beta_source, beta_sign, alpha_slots):
    strings, _, cols = coeffs.shape
    pairs = integrals.shape[0]
    blocks = alpha_slots.shape[1]
    own = coeffs.reshape(strings * 2, cols)
    all_cols = lax.all_to_all(jnp.broadcast_to(own[None], (8, *own.shape)), ("x", "core"), 0, 0, tiled=True)
    counts = pl.pallas_call(
        slot_kernel, out_shape=jax.ShapeDtypeStruct((strings, blocks * strings, 512), BF16), name="slot_counts"
    )(alpha_slots[0])
    dvec = pl.pallas_call(
        gather_kernel,
        out_shape=jax.ShapeDtypeStruct((pairs, 2 * strings * cols), BF16),
        scratch_shapes=[pltpu.VMEM((8, 2 * strings, cols), F32)],
        name="dvec_gather",
    )(all_cols, beta_source, beta_sign)
    parts = pl.pallas_call(
        sum_kernel,
        out_shape=jax.ShapeDtypeStruct((blocks * strings, 2 * cols), BF16),
        scratch_shapes=[pltpu.VMEM((pairs, 2 * strings * cols), BF16)],
        name="slot_sums",
    )(integrals, dvec, counts)
    pieces = lax.all_to_all(parts.reshape(4, 16, strings, 2 * cols), "y", 0, 0, tiled=True)
    half = jnp.sum(pieces.astype(F32), axis=0).astype(BF16)
    pieces = lax.all_to_all(half, "z", 0, 0, tiled=True)
    return jnp.sum(pieces.astype(F32), axis=0).reshape(strings, 2, cols)


def solution(mesh):
    fine = Mesh(mesh.devices.reshape(4, 16, 4, 2), ("y", "z", "x", "core"))
    a, b = ("y", "z"), ("x", "core")
    in_specs = (P(a, None, b), P(), P(None, b), P(None, b), P(a, None, None, None))
    return jax.shard_map(local, mesh=fine, in_specs=in_specs, out_specs=P(a, None, b), check_vma=False)
```

```python
import jax
import jax.numpy as jnp
from jax import lax
from jax.experimental import pallas as pl
from jax.experimental.pallas import tpu as pltpu
from jax.sharding import Mesh
from jax.sharding import PartitionSpec as P

BF16 = jnp.bfloat16
F32 = jnp.float32
I32 = jnp.int32
LANES = 128


def shrink_steps(y, steps, *others):
    for step in steps:
        small = y < 8.0 * 2.0**-step
        y = y * jnp.where(small, 2.0**step, 1.0)
        others = tuple((v * jnp.where(small, 2.0 ** (step * way), 1.0), way) for v, way in others)
    return y, [v for v, _ in others]


def encode(c_ref, c32_ref, tab_ref):
    blocks = c_ref.shape[0]
    strings = tab_ref.shape[1]
    high = None
    for j in range(blocks):
        v = c_ref[j].astype(F32)
        c32_ref[j] = v
        m = jnp.maximum(jnp.abs(v[:strings]), jnp.abs(v[strings:]))
        high = m if high is None else jnp.maximum(high, m)
    high = jnp.broadcast_to(jnp.max(high, axis=(0, 1), keepdims=True), (strings, LANES))
    one = jnp.ones((strings, LANES), F32)
    _, (scale, back) = shrink_steps(high, (64, 32, 16, 8, 4, 2, 1), (one, 1), (one, -1))
    for j in range(blocks):
        re = c32_ref[j, pl.ds(0, strings, stride=2), :] * scale
        im = c32_ref[j, pl.ds(1, strings, stride=2), :] * scale
        size = jnp.maximum(jnp.abs(re), jnp.abs(im))
        power = jnp.zeros((strings, LANES), I32)
        for step in (16, 8, 4, 2, 1):
            small = size < 8.0 * 2.0**-step
            up = jnp.where(small, 2.0**step, 1.0)
            size, re, im = size * up, re * up, im * up
            power = power + jnp.where(small, step, 0)
        low = ((im * 512.0).astype(I32) & 8191) << 6 | power
        top = (re * 2.0**28).astype(I32)
        tab_ref[j] = ((top - low + (1 << 18)) >> 19) << 19 | low
    return back * 2.0**-28


def gather_rows(tab_ref, idx_ref, sgn_ref, d_ref, factor, p0, n):
    blocks, strings, _ = tab_ref.shape
    parts = []
    for r in range(0, n, 8):
        k = min(8, n - r)
        idx = idx_ref[pl.ds(p0 + r, k), :]
        hi = lax.shift_right_logical(idx, 7)
        sign = sgn_ref[pl.ds(p0 + r, k), :].astype(F32) * factor[:k]
        parts.append((sign, idx & (LANES - 1), [hi == j for j in range(blocks)]))
    for a in range(strings):
        got = [None] * len(parts)
        for j in range(blocks):
            for q, (_, lo, here) in enumerate(parts):
                row = jnp.broadcast_to(tab_ref[j, a : a + 1, :], lo.shape)
                v = jnp.take_along_axis(row, lo, axis=1, mode="promise_in_bounds")
                got[q] = v if got[q] is None else jnp.where(here[j], v, got[q])
        values = []
        for v, (sign, _, _) in zip(got, parts):
            power = v & 31
            values.append(((v >> power).astype(F32) * sign, ((v << 13) >> power).astype(F32) * sign))
        for c in range(2):
            v = jnp.concatenate([pair[c] for pair in values], axis=0) if len(values) > 1 else values[0][c]
            at = (a * 2 + c) * LANES
            d_ref[pl.ds(p0, n), at : at + LANES] = v.astype(BF16)


def sigma_kernel(c_ref, idx_ref, sgn_ref, v_ref, m_hbm, o_ref, c32_ref, tab_ref, d_ref, e_ref, m_ref, sem):
    fetch = pltpu.make_async_copy(m_hbm, m_ref, sem)
    fetch.start()
    pairs = v_ref.shape[0]
    strings = tab_ref.shape[1]
    factor = encode(c_ref, c32_ref, tab_ref)

    def body(i, carry):
        gather_rows(tab_ref, idx_ref, sgn_ref, d_ref, carry, pl.multiple_of(i * 16, 16), 16)
        return carry

    factor = lax.fori_loop(0, pairs // 16, body, factor)
    if pairs % 16:
        gather_rows(tab_ref, idx_ref, sgn_ref, d_ref, factor, pairs // 16 * 16, pairs % 16)
    width = 2 * LANES
    for h in range(0, strings, 2):
        at = slice(h * width, (h + 2) * width)
        e_ref[:, at] = jnp.dot(v_ref[...], d_ref[:, at], preferred_element_type=F32).astype(BF16)
    fetch.wait()
    acc = None
    for a in range(strings):
        t = jnp.dot(m_ref[a, :, 0:pairs], e_ref[:, a * width : (a + 1) * width], preferred_element_type=F32)
        acc = t if acc is None else acc + t
    o_ref[...] = acc.astype(BF16)


def slot_kernel(s_ref, m_ref):
    width = m_ref.shape[2]
    rows = lax.broadcasted_iota(I32, (128, 128), 0)
    krow = lax.broadcasted_iota(I32, (width, 128), 0)
    for i in range(s_ref.shape[0] // 2):
        picks, pairs = [], []
        for e in range(2):
            d = i * 2 + e
            code = s_ref[d, 0:1, :] * 16 + e * 8 + s_ref[d, 2:3, :]
            picks.append(jnp.where(rows == code, s_ref[d, 3:4, :].astype(F32), 0.0).astype(BF16))
            pairs.append(jnp.where(krow == s_ref[d, 1:2, :], 1.0, 0.0).astype(BF16))
        m = lax.dot_general(
            jnp.concatenate(picks, axis=1),
            jnp.concatenate(pairs, axis=1),
            (((1,), (1,)), ((), ())),
            preferred_element_type=F32,
        ).astype(BF16)
        for a in range(8):
            m_ref[a, i * 16 : (i + 1) * 16, :] = m[a * 16 : (a + 1) * 16, :]


def local(coeffs, integrals, beta_source, beta_sign, alpha_slots):
    strings, _, cols = coeffs.shape
    pairs = integrals.shape[0]
    blocks = alpha_slots.shape[1]
    step = 16
    vmem = pl.BlockSpec(memory_space=pltpu.VMEM)
    own = coeffs.reshape(strings * 2, cols)
    all_cols = lax.all_to_all(jnp.broadcast_to(own[None], (8, *own.shape)), ("x", "core"), 0, 0, tiled=True)
    counts = pl.pallas_call(
        slot_kernel,
        grid=(blocks // step,),
        in_specs=[pl.BlockSpec((step, 4, 128), lambda i: (i, 0, 0))],
        out_specs=pl.BlockSpec((strings, step * strings, 512), lambda i: (0, i, 0)),
        out_shape=jax.ShapeDtypeStruct((strings, blocks * strings, 512), BF16),
        name="slot_counts",
    )(alpha_slots[0])
    parts = pl.pallas_call(
        sigma_kernel,
        in_specs=[vmem, vmem, vmem, vmem, pl.BlockSpec(memory_space=pl.ANY)],
        out_specs=vmem,
        out_shape=jax.ShapeDtypeStruct((blocks * strings, 2 * cols), BF16),
        scratch_shapes=[
            pltpu.VMEM((8, 2 * strings, cols), F32),
            pltpu.VMEM((8, strings, cols), I32),
            pltpu.VMEM((pairs, 2 * strings * cols), BF16),
            pltpu.VMEM((pairs, 2 * strings * cols), BF16),
            pltpu.VMEM((strings, blocks * strings, 512), BF16),
            pltpu.SemaphoreType.DMA,
        ],
        name="sigma_parts",
    )(all_cols, beta_source, beta_sign, integrals, counts)
    pieces = lax.all_to_all(parts.reshape(4, 16, strings, 2 * cols), "y", 0, 0, tiled=True)
    half = jnp.sum(pieces.astype(F32), axis=0).astype(BF16)
    pieces = lax.all_to_all(half, "z", 0, 0, tiled=True)
    return jnp.sum(pieces.astype(F32), axis=0).reshape(strings, 2, cols)


def solution(mesh):
    fine = Mesh(mesh.devices.reshape(4, 16, 4, 2), ("y", "z", "x", "core"))
    a, b = ("y", "z"), ("x", "core")
    in_specs = (P(a, None, b), P(), P(None, b), P(None, b), P(a, None, None, None))
    return jax.shard_map(local, mesh=fine, in_specs=in_specs, out_specs=P(a, None, b), check_vma=False)
```

```python
import jax
import jax.numpy as jnp
from jax import lax
from jax.experimental import pallas as pl
from jax.experimental.pallas import tpu as pltpu
from jax.sharding import Mesh
from jax.sharding import PartitionSpec as P

BF16 = jnp.bfloat16
F32 = jnp.float32
I32 = jnp.int32
I16 = jnp.int16
LANES = 128


def shrink_steps(y, steps, *others):
    for step in steps:
        small = y < 8.0 * 2.0**-step
        y = y * jnp.where(small, 2.0**step, 1.0)
        others = tuple((v * jnp.where(small, 2.0 ** (step * way), 1.0), way) for v, way in others)
    return y, [v for v, _ in others]


def encode(c_ref, c32_ref, tab_ref):
    blocks = c_ref.shape[0]
    strings = tab_ref.shape[1]
    high = None
    for j in range(blocks):
        v = c_ref[j].astype(F32)
        c32_ref[j] = v
        m = jnp.maximum(jnp.abs(v[:strings]), jnp.abs(v[strings:]))
        high = m if high is None else jnp.maximum(high, m)
    high = jnp.broadcast_to(jnp.max(high, axis=(0, 1), keepdims=True), (strings, LANES))
    one = jnp.ones((strings, LANES), F32)
    _, (scale, back) = shrink_steps(high, (64, 32, 16, 8, 4, 2, 1), (one, 1), (one, -1))
    for j in range(blocks):
        re = c32_ref[j, pl.ds(0, strings, stride=2), :] * scale
        im = c32_ref[j, pl.ds(1, strings, stride=2), :] * scale
        size = jnp.maximum(jnp.abs(re), jnp.abs(im))
        power = jnp.zeros((strings, LANES), I32)
        for step in (16, 8, 4, 2, 1):
            small = size < 8.0 * 2.0**-step
            up = jnp.where(small, 2.0**step, 1.0)
            size, re, im = size * up, re * up, im * up
            power = power + jnp.where(small, step, 0)
        low = ((im * 512.0).astype(I32) & 8191) << 6 | power
        top = (re * 2.0**28).astype(I32)
        tab_ref[j] = ((top - low + (1 << 18)) >> 19) << 19 | low
    return back * 2.0**-28


def gather_rows(tab_ref, idx_ref, sgn_ref, d_ref, factor, p0, n):
    blocks, strings, _ = tab_ref.shape
    parts = []
    for r in range(0, n, 8):
        k = min(8, n - r)
        idx = idx_ref[pl.ds(p0 + r, k), :]
        hi = lax.shift_right_logical(idx, 7)
        sign = sgn_ref[pl.ds(p0 + r, k), :].astype(F32) * factor[:k]
        parts.append((sign, idx & (LANES - 1), [hi == j for j in range(blocks)]))
    for a in range(strings):
        got = [None] * len(parts)
        for j in range(blocks):
            for q, (_, lo, here) in enumerate(parts):
                row = jnp.broadcast_to(tab_ref[j, a : a + 1, :], lo.shape)
                v = jnp.take_along_axis(row, lo, axis=1, mode="promise_in_bounds")
                got[q] = v if got[q] is None else jnp.where(here[j], v, got[q])
        values = []
        for v, (sign, _, _) in zip(got, parts):
            power = v & 31
            values.append(((v >> power).astype(F32) * sign, ((v << 13) >> power).astype(F32) * sign))
        for c in range(2):
            v = jnp.concatenate([pair[c] for pair in values], axis=0) if len(values) > 1 else values[0][c]
            at = (a * 2 + c) * LANES
            d_ref[pl.ds(p0, n), at : at + LANES] = v.astype(BF16)


def slot_kernel(s_ref, m_ref):
    width = m_ref.shape[2]
    rows = lax.broadcasted_iota(I32, (128, 128), 0).astype(I16)
    krow = lax.broadcasted_iota(I32, (width, 128), 0).astype(I16)
    one, zero = jnp.ones((width, 128), BF16), jnp.zeros((width, 128), BF16)
    for d in range(0, s_ref.shape[0], 2):
        picks, pairs = [], []
        for e in range(2):
            code = s_ref[d + e, 0:1, :] * 16 + e * 8 + s_ref[d + e, 2:3, :]
            sign = jnp.broadcast_to(s_ref[d + e, 3:4, :].astype(F32), (128, 128)).astype(BF16)
            picks.append(jnp.where(rows == jnp.broadcast_to(code, (128, 128)).astype(I16), sign, zero[:128]))
            pair = jnp.broadcast_to(s_ref[d + e, 1:2, :], (16, 128)).astype(I16)
            pairs.append(jnp.where(krow == jnp.concatenate([pair] * (width // 16), axis=0), one, zero))
        m = lax.dot_general(
            jnp.concatenate(picks, axis=1),
            jnp.concatenate(pairs, axis=1),
            (((1,), (1,)), ((), ())),
            preferred_element_type=F32,
        ).astype(BF16)
        for a in range(8):
            m_ref[a, d * 8 : d * 8 + 16, :] = m[a * 16 : (a + 1) * 16, :]


def sigma_kernel(c_ref, idx_ref, sgn_ref, v_ref, m_hbm, o_ref, c32_ref, tab_ref, d_ref, e_ref, m_ref, sem):
    fetch = pltpu.make_async_copy(m_hbm, m_ref, sem)
    fetch.start()
    pairs = v_ref.shape[0]
    strings = tab_ref.shape[1]
    factor = encode(c_ref, c32_ref, tab_ref)

    def body(i, carry):
        gather_rows(tab_ref, idx_ref, sgn_ref, d_ref, carry, pl.multiple_of(i * 16, 16), 16)
        return carry

    factor = lax.fori_loop(0, pairs // 16, body, factor)
    if pairs % 16:
        gather_rows(tab_ref, idx_ref, sgn_ref, d_ref, factor, pairs // 16 * 16, pairs % 16)
    width = 2 * LANES
    for h in range(0, strings, 2):
        at = slice(h * width, (h + 2) * width)
        e_ref[:, at] = jnp.dot(v_ref[...], d_ref[:, at], preferred_element_type=F32).astype(BF16)
    fetch.wait()
    acc = None
    for a in range(strings):
        t = jnp.dot(m_ref[a, :, 0:pairs], e_ref[:, a * width : (a + 1) * width], preferred_element_type=F32)
        acc = t if acc is None else acc + t
    o_ref[...] = acc.astype(BF16)


def local(coeffs, integrals, beta_source, beta_sign, alpha_slots):
    strings, _, cols = coeffs.shape
    pairs = integrals.shape[0]
    blocks = alpha_slots.shape[1]
    step = 16
    vmem = pl.BlockSpec(memory_space=pltpu.VMEM)
    own = coeffs.reshape(strings * 2, cols)
    all_cols = lax.all_to_all(jnp.broadcast_to(own[None], (8, *own.shape)), ("x", "core"), 0, 0, tiled=True)
    counts = pl.pallas_call(
        slot_kernel,
        grid=(blocks // step,),
        in_specs=[pl.BlockSpec((step, 4, 128), lambda i: (i, 0, 0))],
        out_specs=pl.BlockSpec((strings, step * strings, 512), lambda i: (0, i, 0)),
        out_shape=jax.ShapeDtypeStruct((strings, blocks * strings, 512), BF16),
        name="slot_counts",
    )(alpha_slots[0])
    parts = pl.pallas_call(
        sigma_kernel,
        in_specs=[vmem] * 4 + [pl.BlockSpec(memory_space=pl.ANY)],
        out_specs=vmem,
        out_shape=jax.ShapeDtypeStruct((blocks * strings, 2 * cols), BF16),
        scratch_shapes=[
            pltpu.VMEM((8, 2 * strings, cols), F32),
            pltpu.VMEM((8, strings, cols), I32),
            pltpu.VMEM((pairs, 2 * strings * cols), BF16),
            pltpu.VMEM((pairs, 2 * strings * cols), BF16),
            pltpu.VMEM((strings, blocks * strings, 512), BF16),
            pltpu.SemaphoreType.DMA,
        ],
        name="sigma_parts",
    )(*[pltpu.with_memory_space_constraint(x, pltpu.VMEM) for x in (all_cols, beta_source, beta_sign, integrals)], counts)
    pieces = lax.all_to_all(parts.reshape(4, 16, strings, 2 * cols), "y", 0, 0, tiled=True)
    half = jnp.sum(pieces.astype(F32), axis=0).astype(BF16)
    pieces = lax.all_to_all(half, "z", 0, 0, tiled=True)
    return jnp.sum(pieces.astype(F32), axis=0).reshape(strings, 2, cols)


def solution(mesh):
    fine = Mesh(mesh.devices.reshape(4, 16, 4, 2), ("y", "z", "x", "core"))
    a, b = ("y", "z"), ("x", "core")
    in_specs = (P(a, None, b), P(), P(None, b), P(None, b), P(a, None, None, None))
    return jax.shard_map(local, mesh=fine, in_specs=in_specs, out_specs=P(a, None, b), check_vma=False)
```

```python
import jax
import jax.numpy as jnp
from jax import lax
from jax.experimental import pallas as pl
from jax.experimental.pallas import tpu as pltpu
from jax.sharding import Mesh
from jax.sharding import PartitionSpec as P

BF16 = jnp.bfloat16
F32 = jnp.float32
I32 = jnp.int32
I16 = jnp.int16
LANES = 128
UNROLL = 8


def shrink_steps(y, steps, *others):
    for step in steps:
        small = y < 8.0 * 2.0**-step
        y = y * jnp.where(small, 2.0**step, 1.0)
        others = tuple((v * jnp.where(small, 2.0 ** (step * way), 1.0), way) for v, way in others)
    return y, [v for v, _ in others]


def encode(c_ref, c32_ref, tab_ref):
    blocks = c_ref.shape[0]
    strings = tab_ref.shape[1]
    high = None
    for j in range(blocks):
        v = c_ref[j].astype(F32)
        c32_ref[j] = v
        m = jnp.maximum(jnp.abs(v[:strings]), jnp.abs(v[strings:]))
        high = m if high is None else jnp.maximum(high, m)
    high = jnp.broadcast_to(jnp.max(high, axis=(0, 1), keepdims=True), (strings, LANES))
    one = jnp.ones((strings, LANES), F32)
    _, (scale, back) = shrink_steps(high, (64, 32, 16, 8, 4, 2, 1), (one, 1), (one, -1))
    for j in range(blocks):
        re = c32_ref[j, pl.ds(0, strings, stride=2), :] * scale
        im = c32_ref[j, pl.ds(1, strings, stride=2), :] * scale
        size = jnp.maximum(jnp.abs(re), jnp.abs(im))
        power = jnp.zeros((strings, LANES), I32)
        for step in (16, 8, 4, 2, 1):
            small = size < 8.0 * 2.0**-step
            up = jnp.where(small, 2.0**step, 1.0)
            size, re, im = size * up, re * up, im * up
            power = power + jnp.where(small, step, 0)
        low = ((im * 512.0).astype(I32) & 8191) << 6 | power
        top = (re * 2.0**28).astype(I32)
        tab_ref[j] = ((top - low + (1 << 18)) >> 19) << 19 | low
    return back * 2.0**-28


def gather_rows(tab_ref, idx_ref, sgn_ref, d_ref, factor, p0, n):
    blocks, strings, _ = tab_ref.shape
    parts = []
    for r in range(0, n, 8):
        k = min(8, n - r)
        idx = idx_ref[pl.ds(p0 + r, k), :]
        hi = lax.shift_right_logical(idx, 7)
        sign = sgn_ref[pl.ds(p0 + r, k), :].astype(F32) * factor[:k]
        parts.append((sign, idx & (LANES - 1), [hi == j for j in range(blocks)]))
    for a in range(strings):
        got = [None] * len(parts)
        for j in range(blocks):
            for q, (_, lo, here) in enumerate(parts):
                row = jnp.broadcast_to(tab_ref[j, a : a + 1, :], lo.shape)
                v = jnp.take_along_axis(row, lo, axis=1, mode="promise_in_bounds")
                got[q] = v if got[q] is None else jnp.where(here[j], v, got[q])
        values = []
        for v, (sign, _, _) in zip(got, parts):
            power = v & 31
            values.append(((v >> power).astype(F32) * sign, ((v << 13) >> power).astype(F32) * sign))
        for c in range(2):
            v = jnp.concatenate([pair[c] for pair in values], axis=0) if len(values) > 1 else values[0][c]
            at = (a * 2 + c) * LANES
            d_ref[pl.ds(p0, n), at : at + LANES] = v.astype(BF16)


def slot_kernel(s_ref, idx_hbm, sgn_hbm, first_hbm, m_ref, idx_ref, sgn_ref, half_ref, sems):
    fetches = [pltpu.make_async_copy(idx_hbm, idx_ref, sems.at[1]), pltpu.make_async_copy(sgn_hbm, sgn_ref, sems.at[2])]
    for fetch in fetches:
        fetch.start()
    width = m_ref.shape[2]
    rows = lax.broadcasted_iota(I32, (128, 128), 0).astype(I16)
    krow = lax.broadcasted_iota(I32, (width, 128), 0).astype(I16)
    one, zero = jnp.ones((width, 128), BF16), jnp.zeros((width, 128), BF16)

    def pair_of_blocks(d, out_ref, row):
        picks, pairs = [], []
        for e in range(2):
            code = s_ref[d + e, 0:1, :] * 16 + e * 8 + s_ref[d + e, 2:3, :]
            sign = jnp.broadcast_to(s_ref[d + e, 3:4, :].astype(F32), (128, 128)).astype(BF16)
            picks.append(jnp.where(rows == jnp.broadcast_to(code, (128, 128)).astype(I16), sign, zero[:128]))
            pair = jnp.broadcast_to(s_ref[d + e, 1:2, :], (16, 128)).astype(I16)
            pairs.append(jnp.where(krow == jnp.concatenate([pair] * (width // 16), axis=0), one, zero))
        m = lax.dot_general(
            jnp.concatenate(picks, axis=1),
            jnp.concatenate(pairs, axis=1),
            (((1,), (1,)), ((), ())),
            preferred_element_type=F32,
        ).astype(BF16)
        for a in range(8):
            out_ref[a, pl.ds(pl.multiple_of(row, 16), 16), :] = m[a * 16 : (a + 1) * 16, :]

    half = s_ref.shape[0] // 2

    def count(first, out_ref):
        def body(i, carry):
            for d in range(0, UNROLL, 2):
                pair_of_blocks(first + i * UNROLL + d, out_ref, (i * UNROLL + d) * 8)
            return carry

        lax.fori_loop(0, half // UNROLL, body, 0)

    count(0, half_ref)
    send = pltpu.make_async_copy(half_ref, first_hbm, sems.at[0])
    send.start()
    count(half, m_ref)
    send.wait()
    for fetch in fetches:
        fetch.wait()


def sigma_kernel(c_ref, idx_ref, sgn_ref, second_ref, v_hbm, first_hbm, o_ref, c32_ref, tab_ref, d_ref, e_ref, m_ref, v_ref, sems):
    half = second_ref.shape[1]
    fetches = [
        pltpu.make_async_copy(first_hbm, m_ref.at[:, :half, :], sems.at[0]),
        pltpu.make_async_copy(second_ref, m_ref.at[:, half:, :], sems.at[1]),
        pltpu.make_async_copy(v_hbm, v_ref, sems.at[2]),
    ]
    for fetch in fetches:
        fetch.start()
    pairs = v_ref.shape[0]
    strings = tab_ref.shape[1]
    factor = encode(c_ref, c32_ref, tab_ref)

    def body(i, carry):
        gather_rows(tab_ref, idx_ref, sgn_ref, d_ref, carry, pl.multiple_of(i * 16, 16), 16)
        return carry

    factor = lax.fori_loop(0, pairs // 16, body, factor)
    if pairs % 16:
        gather_rows(tab_ref, idx_ref, sgn_ref, d_ref, factor, pairs // 16 * 16, pairs % 16)
    for fetch in fetches:
        fetch.wait()
    width = 2 * LANES
    for h in range(0, strings, 2):
        at = slice(h * width, (h + 2) * width)
        e_ref[:, at] = jnp.dot(v_ref[...], d_ref[:, at], preferred_element_type=F32).astype(BF16)
    acc = None
    for a in range(strings):
        t = jnp.dot(m_ref[a, :, 0:pairs], e_ref[:, a * width : (a + 1) * width], preferred_element_type=F32)
        acc = t if acc is None else acc + t
    o_ref[...] = acc.astype(BF16)


def local(coeffs, integrals, beta_source, beta_sign, alpha_slots):
    strings, _, cols = coeffs.shape
    pairs = integrals.shape[0]
    blocks = alpha_slots.shape[1]
    vmem = pl.BlockSpec(memory_space=pltpu.VMEM)
    own = coeffs.reshape(strings * 2, cols)
    all_cols = lax.all_to_all(jnp.broadcast_to(own[None], (8, *own.shape)), ("x", "core"), 0, 0, tiled=True)
    def in_vmem(x):
        return pltpu.with_memory_space_constraint(x, pltpu.VMEM)

    def in_hbm(x):
        return pltpu.with_memory_space_constraint(x, pltpu.HBM)

    half = (strings, blocks * strings // 2, 512)
    hbm = pl.BlockSpec(memory_space=pltpu.HBM)
    first, second, source, sign = pl.pallas_call(
        slot_kernel,
        in_specs=[vmem, hbm, hbm],
        out_specs=[hbm, vmem, vmem, vmem],
        out_shape=[pltpu.HBM(half, BF16), pltpu.VMEM(half, BF16)] + [pltpu.VMEM((pairs, cols), I32)] * 2,
        scratch_shapes=[pltpu.VMEM(half, BF16), pltpu.SemaphoreType.DMA((3,))],
        compiler_params=pltpu.CompilerParams(vmem_limit_bytes=24 << 20),
        name="slot_counts",
    )(in_vmem(alpha_slots[0]), in_hbm(beta_source), in_hbm(beta_sign))
    parts = pl.pallas_call(
        sigma_kernel,
        in_specs=[vmem] * 4 + [hbm] * 2,
        out_specs=vmem,
        out_shape=jax.ShapeDtypeStruct((blocks * strings, 2 * cols), BF16),
        scratch_shapes=[
            pltpu.VMEM((8, 2 * strings, cols), F32),
            pltpu.VMEM((8, strings, cols), I32),
            pltpu.VMEM((pairs, 2 * strings * cols), BF16),
            pltpu.VMEM((pairs, 2 * strings * cols), BF16),
            pltpu.VMEM((strings, blocks * strings, 512), BF16),
            pltpu.VMEM((pairs, pairs), BF16),
            pltpu.SemaphoreType.DMA((3,)),
        ],
        compiler_params=pltpu.CompilerParams(vmem_limit_bytes=24 << 20),
        name="sigma_parts",
    )(in_vmem(all_cols), source, sign, second, in_hbm(integrals), in_hbm(first))
    pieces = lax.all_to_all(parts.reshape(4, 16, strings, 2 * cols), "y", 0, 0, tiled=True)
    half = jnp.sum(pieces.astype(F32), axis=0).astype(BF16)
    pieces = lax.all_to_all(half, "z", 0, 0, tiled=True)
    return jnp.sum(pieces.astype(F32), axis=0).reshape(strings, 2, cols)


def solution(mesh):
    fine = Mesh(mesh.devices.reshape(4, 16, 4, 2), ("y", "z", "x", "core"))
    a, b = ("y", "z"), ("x", "core")
    in_specs = (P(a, None, b), P(), P(None, b), P(None, b), P(a, None, None, None))
    return jax.shard_map(local, mesh=fine, in_specs=in_specs, out_specs=P(a, None, b), check_vma=False)
```

```python
import jax
import jax.numpy as jnp
from jax import lax
from jax.experimental import pallas as pl
from jax.experimental.pallas import tpu as pltpu
from jax.sharding import Mesh
from jax.sharding import PartitionSpec as P

BF16 = jnp.bfloat16
F32 = jnp.float32
I32 = jnp.int32
I16 = jnp.int16
LANES = 128
UNROLL = 8


def shrink_steps(y, steps, *others):
    for step in steps:
        small = y < 8.0 * 2.0**-step
        y = y * jnp.where(small, 2.0**step, 1.0)
        others = tuple((v * jnp.where(small, 2.0 ** (step * way), 1.0), way) for v, way in others)
    return y, [v for v, _ in others]


def encode(c_ref, c32_ref, tab_ref):
    blocks = c_ref.shape[0]
    strings = tab_ref.shape[1]
    high = None
    for j in range(blocks):
        v = c_ref[j].astype(F32)
        c32_ref[j] = v
        m = jnp.maximum(jnp.abs(v[:strings]), jnp.abs(v[strings:]))
        high = m if high is None else jnp.maximum(high, m)
    high = jnp.broadcast_to(jnp.max(high, axis=(0, 1), keepdims=True), (strings, LANES))
    one = jnp.ones((strings, LANES), F32)
    _, (scale, back) = shrink_steps(high, (64, 32, 16, 8, 4, 2, 1), (one, 1), (one, -1))
    for j in range(blocks):
        re = c32_ref[j, pl.ds(0, strings, stride=2), :] * scale
        im = c32_ref[j, pl.ds(1, strings, stride=2), :] * scale
        size = jnp.maximum(jnp.abs(re), jnp.abs(im))
        power = jnp.zeros((strings, LANES), I32)
        for step in (16, 8, 4, 2, 1):
            small = size < 8.0 * 2.0**-step
            up = jnp.where(small, 2.0**step, 1.0)
            size, re, im = size * up, re * up, im * up
            power = power + jnp.where(small, step, 0)
        low = ((im * 512.0).astype(I32) & 8191) << 6 | power
        top = (re * 2.0**28).astype(I32)
        tab_ref[j] = ((top - low + (1 << 18)) >> 19) << 19 | low
    return back * 2.0**-28


def gather_rows(tab_ref, idx_ref, sgn_ref, d_ref, factor, p0, n):
    blocks, strings, _ = tab_ref.shape
    parts = []
    for r in range(0, n, 8):
        k = min(8, n - r)
        idx = idx_ref[pl.ds(p0 + r, k), :]
        hi = lax.shift_right_logical(idx, 7)
        sign = sgn_ref[pl.ds(p0 + r, k), :].astype(F32) * factor[:k]
        parts.append((sign, idx & (LANES - 1), [hi == j for j in range(blocks)]))
    for a in range(strings):
        got = [None] * len(parts)
        for j in range(blocks):
            for q, (_, lo, here) in enumerate(parts):
                row = jnp.broadcast_to(tab_ref[j, a : a + 1, :], lo.shape)
                v = jnp.take_along_axis(row, lo, axis=1, mode="promise_in_bounds")
                got[q] = v if got[q] is None else jnp.where(here[j], v, got[q])
        values = []
        for v, (sign, _, _) in zip(got, parts):
            power = v & 31
            values.append(((v >> power).astype(F32) * sign, ((v << 13) >> power).astype(F32) * sign))
        for c in range(2):
            v = jnp.concatenate([pair[c] for pair in values], axis=0) if len(values) > 1 else values[0][c]
            at = (a * 2 + c) * LANES
            d_ref[pl.ds(p0, n), at : at + LANES] = v.astype(BF16)


def spread_kernel(own_ref, s_hbm, rep_ref, s_ref, sems):
    count = rep_ref.shape[0]
    copies = [pltpu.make_async_copy(own_ref, rep_ref.at[j], sems.at[j]) for j in range(count)]
    copies.append(pltpu.make_async_copy(s_hbm, s_ref, sems.at[count]))
    for copy in copies:
        copy.start()
    for copy in copies:
        copy.wait()


def slot_kernel(s_ref, idx_hbm, sgn_hbm, first_hbm, m_ref, idx_ref, sgn_ref, half_ref, sems):
    fetches = [pltpu.make_async_copy(idx_hbm, idx_ref, sems.at[1]), pltpu.make_async_copy(sgn_hbm, sgn_ref, sems.at[2])]
    for fetch in fetches:
        fetch.start()
    width = m_ref.shape[2]
    rows = lax.broadcasted_iota(I32, (128, 128), 0).astype(I16)
    krow = lax.broadcasted_iota(I32, (width, 128), 0).astype(I16)
    one, zero = jnp.ones((width, 128), BF16), jnp.zeros((width, 128), BF16)

    def pair_of_blocks(d, out_ref, row):
        picks, pairs = [], []
        for e in range(2):
            code = s_ref[d + e, 0:1, :] * 16 + e * 8 + s_ref[d + e, 2:3, :]
            sign = jnp.broadcast_to(s_ref[d + e, 3:4, :].astype(F32), (128, 128)).astype(BF16)
            picks.append(jnp.where(rows == jnp.broadcast_to(code, (128, 128)).astype(I16), sign, zero[:128]))
            pair = jnp.broadcast_to(s_ref[d + e, 1:2, :], (16, 128)).astype(I16)
            pairs.append(jnp.where(krow == jnp.concatenate([pair] * (width // 16), axis=0), one, zero))
        m = lax.dot_general(
            jnp.concatenate(picks, axis=1),
            jnp.concatenate(pairs, axis=1),
            (((1,), (1,)), ((), ())),
            preferred_element_type=F32,
        ).astype(BF16)
        for a in range(8):
            out_ref[a, pl.ds(pl.multiple_of(row, 16), 16), :] = m[a * 16 : (a + 1) * 16, :]

    half = s_ref.shape[0] // 2

    def count(first, out_ref):
        def body(i, carry):
            for d in range(0, UNROLL, 2):
                pair_of_blocks(first + i * UNROLL + d, out_ref, (i * UNROLL + d) * 8)
            return carry

        lax.fori_loop(0, half // UNROLL, body, 0)

    count(0, half_ref)
    send = pltpu.make_async_copy(half_ref, first_hbm, sems.at[0])
    send.start()
    count(half, m_ref)
    send.wait()
    for fetch in fetches:
        fetch.wait()


def sigma_kernel(c_ref, idx_ref, sgn_ref, second_ref, v_hbm, first_hbm, o_ref, c32_ref, tab_ref, d_ref, e_ref, m_ref, v_ref, sems):
    half = second_ref.shape[1]
    fetches = [
        pltpu.make_async_copy(first_hbm, m_ref.at[:, :half, :], sems.at[0]),
        pltpu.make_async_copy(second_ref, m_ref.at[:, half:, :], sems.at[1]),
        pltpu.make_async_copy(v_hbm, v_ref, sems.at[2]),
    ]
    for fetch in fetches:
        fetch.start()
    pairs = v_ref.shape[0]
    strings = tab_ref.shape[1]
    factor = encode(c_ref, c32_ref, tab_ref)

    def body(i, carry):
        gather_rows(tab_ref, idx_ref, sgn_ref, d_ref, carry, pl.multiple_of(i * 16, 16), 16)
        return carry

    factor = lax.fori_loop(0, pairs // 16, body, factor)
    if pairs % 16:
        gather_rows(tab_ref, idx_ref, sgn_ref, d_ref, factor, pairs // 16 * 16, pairs % 16)
    for fetch in fetches:
        fetch.wait()
    width = 2 * LANES
    for h in range(0, strings, 2):
        at = slice(h * width, (h + 2) * width)
        e_ref[:, at] = jnp.dot(v_ref[...], d_ref[:, at], preferred_element_type=F32).astype(BF16)
    acc = None
    for a in range(strings):
        t = jnp.dot(m_ref[a, :, 0:pairs], e_ref[:, a * width : (a + 1) * width], preferred_element_type=F32)
        acc = t if acc is None else acc + t
    o_ref[...] = acc.astype(BF16)


def local(coeffs, integrals, beta_source, beta_sign, alpha_slots):
    strings, _, cols = coeffs.shape
    pairs = integrals.shape[0]
    blocks = alpha_slots.shape[1]
    vmem = pl.BlockSpec(memory_space=pltpu.VMEM)
    def in_vmem(x):
        return pltpu.with_memory_space_constraint(x, pltpu.VMEM)

    def in_hbm(x):
        return pltpu.with_memory_space_constraint(x, pltpu.HBM)

    hbm = pl.BlockSpec(memory_space=pltpu.HBM)
    own = coeffs.reshape(strings * 2, cols)
    spread, slots = pl.pallas_call(
        spread_kernel,
        in_specs=[hbm, hbm],
        out_specs=[pl.BlockSpec(memory_space=pl.ANY), vmem],
        out_shape=[jax.ShapeDtypeStruct((8, *own.shape), BF16), pltpu.VMEM(alpha_slots.shape[1:], I32)],
        scratch_shapes=[pltpu.SemaphoreType.DMA((9,))],
        compiler_params=pltpu.CompilerParams(vmem_limit_bytes=24 << 20),
        name="spread",
    )(in_hbm(own), in_hbm(alpha_slots[0]))
    all_cols = lax.all_to_all(spread, ("x", "core"), 0, 0, tiled=True)
    half = (strings, blocks * strings // 2, 512)
    first, second, source, sign = pl.pallas_call(
        slot_kernel,
        in_specs=[vmem, hbm, hbm],
        out_specs=[hbm, vmem, vmem, vmem],
        out_shape=[pltpu.HBM(half, BF16), pltpu.VMEM(half, BF16)] + [pltpu.VMEM((pairs, cols), I32)] * 2,
        scratch_shapes=[pltpu.VMEM(half, BF16), pltpu.SemaphoreType.DMA((3,))],
        compiler_params=pltpu.CompilerParams(vmem_limit_bytes=24 << 20),
        name="slot_counts",
    )(slots, in_hbm(beta_source), in_hbm(beta_sign))
    parts = pl.pallas_call(
        sigma_kernel,
        in_specs=[vmem] * 4 + [hbm] * 2,
        out_specs=vmem,
        out_shape=jax.ShapeDtypeStruct((blocks * strings, 2 * cols), BF16),
        scratch_shapes=[
            pltpu.VMEM((8, 2 * strings, cols), F32),
            pltpu.VMEM((8, strings, cols), I32),
            pltpu.VMEM((pairs, 2 * strings * cols), BF16),
            pltpu.VMEM((pairs, 2 * strings * cols), BF16),
            pltpu.VMEM((strings, blocks * strings, 512), BF16),
            pltpu.VMEM((pairs, pairs), BF16),
            pltpu.SemaphoreType.DMA((3,)),
        ],
        compiler_params=pltpu.CompilerParams(vmem_limit_bytes=24 << 20),
        name="sigma_parts",
    )(in_vmem(all_cols), source, sign, second, in_hbm(integrals), in_hbm(first))
    pieces = lax.all_to_all(parts.reshape(4, 16, strings, 2 * cols), "y", 0, 0, tiled=True)
    half = jnp.sum(pieces.astype(F32), axis=0).astype(BF16)
    pieces = lax.all_to_all(half, "z", 0, 0, tiled=True)
    return jnp.sum(pieces.astype(F32), axis=0).reshape(strings, 2, cols)


def solution(mesh):
    fine = Mesh(mesh.devices.reshape(4, 16, 4, 2), ("y", "z", "x", "core"))
    a, b = ("y", "z"), ("x", "core")
    in_specs = (P(a, None, b), P(), P(None, b), P(None, b), P(a, None, None, None))
    return jax.shard_map(local, mesh=fine, in_specs=in_specs, out_specs=P(a, None, b), check_vma=False)
```

```python
import jax
import jax.numpy as jnp
from jax import lax
from jax.experimental import pallas as pl
from jax.experimental.pallas import tpu as pltpu
from jax.sharding import Mesh
from jax.sharding import PartitionSpec as P

BF16 = jnp.bfloat16
F32 = jnp.float32
I32 = jnp.int32
I16 = jnp.int16
LANES = 128
UNROLL = 8
ROWS = 160


def shrink_steps(y, steps, *others):
    for step in steps:
        small = y < 8.0 * 2.0**-step
        y = y * jnp.where(small, 2.0**step, 1.0)
        others = tuple((v * jnp.where(small, 2.0 ** (step * way), 1.0), way) for v, way in others)
    return y, [v for v, _ in others]


def encode(c_ref, c32_ref, tab_ref):
    blocks = c_ref.shape[0]
    strings = tab_ref.shape[1]
    high = None
    for j in range(blocks):
        v = c_ref[j].astype(F32)
        c32_ref[j] = v
        m = jnp.maximum(jnp.abs(v[:strings]), jnp.abs(v[strings:]))
        high = m if high is None else jnp.maximum(high, m)
    high = jnp.broadcast_to(jnp.max(high, axis=(0, 1), keepdims=True), (strings, LANES))
    one = jnp.ones((strings, LANES), F32)
    _, (scale, back) = shrink_steps(high, (64, 32, 16, 8, 4, 2, 1), (one, 1), (one, -1))
    for j in range(blocks):
        re = c32_ref[j, pl.ds(0, strings, stride=2), :] * scale
        im = c32_ref[j, pl.ds(1, strings, stride=2), :] * scale
        size = jnp.maximum(jnp.abs(re), jnp.abs(im))
        power = jnp.zeros((strings, LANES), I32)
        for step in (16, 8, 4, 2, 1):
            small = size < 8.0 * 2.0**-step
            up = jnp.where(small, 2.0**step, 1.0)
            size, re, im = size * up, re * up, im * up
            power = power + jnp.where(small, step, 0)
        low = ((im * 512.0).astype(I32) & 8191) << 6 | power
        top = (re * 2.0**28).astype(I32)
        tab_ref[j] = ((top - low + (1 << 18)) >> 19) << 19 | low
    return back * 2.0**-28


def gather_block(tab_ref, idx_ref, sgn_ref, factor, p0, n):
    blocks, strings, _ = tab_ref.shape
    idx = idx_ref[pl.ds(p0, n), :]
    sign = sgn_ref[pl.ds(p0, n), :].astype(F32) * factor[:n]
    hi = lax.shift_right_logical(idx, 7)
    lo = idx & (LANES - 1)
    here = [hi == j for j in range(blocks)]
    values = []
    for a in range(0, strings, 2):
        got = [None, None]
        for j in range(blocks):
            for q in range(2):
                row = jnp.broadcast_to(tab_ref[j, a + q : a + q + 1, :], lo.shape)
                v = jnp.take_along_axis(row, lo, axis=1, mode="promise_in_bounds")
                got[q] = v if got[q] is None else jnp.where(here[j], v, got[q])
        for v in got:
            power = v & 31
            values.append(((v >> power).astype(F32) * sign, ((v << 13) >> power).astype(F32) * sign))
    return values


def gather_rows(tab_ref, idx_ref, sgn_ref, d_ref, factor, p0, n):
    parts = [gather_block(tab_ref, idx_ref, sgn_ref, factor, p0 + r, min(8, n - r)) for r in range(0, n, 8)]
    for a in range(tab_ref.shape[1]):
        for c in range(2):
            v = jnp.concatenate([part[a][c] for part in parts], axis=0) if len(parts) > 1 else parts[0][a][c]
            at = (a * 2 + c) * LANES
            d_ref[pl.ds(p0, n), at : at + LANES] = v.astype(BF16)


def slot_kernel(s_ref, idx_hbm, sgn_hbm, first_hbm, m_ref, idx_ref, sgn_ref, half_ref, sems):
    fetches = [pltpu.make_async_copy(idx_hbm, idx_ref, sems.at[1]), pltpu.make_async_copy(sgn_hbm, sgn_ref, sems.at[2])]
    for fetch in fetches:
        fetch.start()
    width = m_ref.shape[2]
    rows = lax.broadcasted_iota(I32, (128, 128), 0).astype(I16)
    krow = lax.broadcasted_iota(I32, (width, 128), 0).astype(I16)
    one, zero = jnp.ones((width, 128), BF16), jnp.zeros((width, 128), BF16)

    def pair_of_blocks(d, out_ref, row):
        picks, pairs = [], []
        for e in range(2):
            code = s_ref[d + e, 0:1, :] * 16 + e * 8 + s_ref[d + e, 2:3, :]
            sign = jnp.broadcast_to(s_ref[d + e, 3:4, :].astype(F32), (128, 128)).astype(BF16)
            picks.append(jnp.where(rows == jnp.broadcast_to(code, (128, 128)).astype(I16), sign, zero[:128]))
            pair = jnp.broadcast_to(s_ref[d + e, 1:2, :], (16, 128)).astype(I16)
            pairs.append(jnp.where(krow == jnp.concatenate([pair] * (width // 16), axis=0), one, zero))
        m = lax.dot_general(
            jnp.concatenate(picks, axis=1),
            jnp.concatenate(pairs, axis=1),
            (((1,), (1,)), ((), ())),
            preferred_element_type=F32,
        ).astype(BF16)
        for a in range(8):
            out_ref[a, pl.ds(pl.multiple_of(row, 16), 16), :] = m[a * 16 : (a + 1) * 16, :]

    half = s_ref.shape[0] // 2

    def count(first, out_ref):
        def body(i, carry):
            for d in range(0, UNROLL, 2):
                pair_of_blocks(first + i * UNROLL + d, out_ref, (i * UNROLL + d) * 8)
            return carry

        lax.fori_loop(0, half // UNROLL, body, 0)

    count(0, half_ref)
    send = pltpu.make_async_copy(half_ref, first_hbm, sems.at[0])
    send.start()
    count(half, m_ref)
    send.wait()
    for fetch in fetches:
        fetch.wait()


def sigma_kernel(c_ref, idx_ref, sgn_ref, second_ref, v_hbm, first_hbm, o_ref, c32_ref, tab_ref, d_ref, e_ref, m_ref, v_ref, sems):
    half = second_ref.shape[1]
    fetches = [
        pltpu.make_async_copy(first_hbm, m_ref.at[:, :half, :], sems.at[0]),
        pltpu.make_async_copy(second_ref, m_ref.at[:, half:, :], sems.at[1]),
        pltpu.make_async_copy(v_hbm, v_ref, sems.at[2]),
    ]
    for fetch in fetches:
        fetch.start()
    pairs = v_ref.shape[0]
    strings = tab_ref.shape[1]
    factor = encode(c_ref, c32_ref, tab_ref)

    def body(i, carry):
        for r in range(0, ROWS, 16):
            p0 = pl.multiple_of(i * ROWS + r, 16)
            gather_rows(tab_ref, idx_ref, sgn_ref, d_ref, carry, p0, 16)
        return carry

    factor = lax.fori_loop(0, pairs // ROWS, body, factor)
    for p0 in range(pairs // ROWS * ROWS, pairs, 16):
        gather_rows(tab_ref, idx_ref, sgn_ref, d_ref, factor, p0, min(16, pairs - p0))
    for fetch in fetches:
        fetch.wait()
    width = 2 * LANES
    for h in range(0, strings, 2):
        at = slice(h * width, (h + 2) * width)
        e_ref[:, at] = jnp.dot(v_ref[...], d_ref[:, at], preferred_element_type=F32).astype(BF16)
    acc = None
    for a in range(strings):
        t = jnp.dot(m_ref[a, :, 0:pairs], e_ref[:, a * width : (a + 1) * width], preferred_element_type=F32)
        acc = t if acc is None else acc + t
    o_ref[...] = acc.astype(BF16)


def local(coeffs, integrals, beta_source, beta_sign, alpha_slots):
    strings, _, cols = coeffs.shape
    pairs = integrals.shape[0]
    blocks = alpha_slots.shape[1]
    vmem = pl.BlockSpec(memory_space=pltpu.VMEM)
    own = coeffs.reshape(strings * 2, cols)
    all_cols = lax.all_to_all(jnp.broadcast_to(own[None], (8, *own.shape)), ("x", "core"), 0, 0, tiled=True)
    def in_vmem(x):
        return pltpu.with_memory_space_constraint(x, pltpu.VMEM)

    def in_hbm(x):
        return pltpu.with_memory_space_constraint(x, pltpu.HBM)

    half = (strings, blocks * strings // 2, 512)
    hbm = pl.BlockSpec(memory_space=pltpu.HBM)
    first, second, source, sign = pl.pallas_call(
        slot_kernel,
        in_specs=[vmem, hbm, hbm],
        out_specs=[hbm, vmem, vmem, vmem],
        out_shape=[pltpu.HBM(half, BF16), pltpu.VMEM(half, BF16)] + [pltpu.VMEM((pairs, cols), I32)] * 2,
        scratch_shapes=[pltpu.VMEM(half, BF16), pltpu.SemaphoreType.DMA((3,))],
        compiler_params=pltpu.CompilerParams(vmem_limit_bytes=24 << 20),
        name="slot_counts",
    )(in_vmem(alpha_slots[0]), in_hbm(beta_source), in_hbm(beta_sign))
    parts = pl.pallas_call(
        sigma_kernel,
        in_specs=[vmem] * 4 + [hbm] * 2,
        out_specs=vmem,
        out_shape=jax.ShapeDtypeStruct((blocks * strings, 2 * cols), BF16),
        scratch_shapes=[
            pltpu.VMEM((8, 2 * strings, cols), F32),
            pltpu.VMEM((8, strings, cols), I32),
            pltpu.VMEM((pairs, 2 * strings * cols), BF16),
            pltpu.VMEM((pairs, 2 * strings * cols), BF16),
            pltpu.VMEM((strings, blocks * strings, 512), BF16),
            pltpu.VMEM((pairs, pairs), BF16),
            pltpu.SemaphoreType.DMA((3,)),
        ],
        compiler_params=pltpu.CompilerParams(vmem_limit_bytes=24 << 20),
        name="sigma_parts",
    )(in_vmem(all_cols), source, sign, second, in_hbm(integrals), in_hbm(first))
    pieces = lax.all_to_all(parts.reshape(4, 16, strings, 2 * cols), "y", 0, 0, tiled=True)
    half = jnp.sum(pieces.astype(F32), axis=0).astype(BF16)
    pieces = lax.all_to_all(half, "z", 0, 0, tiled=True)
    return jnp.sum(pieces.astype(F32), axis=0).reshape(strings, 2, cols)


def solution(mesh):
    fine = Mesh(mesh.devices.reshape(4, 16, 4, 2), ("y", "z", "x", "core"))
    a, b = ("y", "z"), ("x", "core")
    in_specs = (P(a, None, b), P(), P(None, b), P(None, b), P(a, None, None, None))
    return jax.shard_map(local, mesh=fine, in_specs=in_specs, out_specs=P(a, None, b), check_vma=False)
```

```python
import jax
import jax.numpy as jnp
from jax import lax
from jax.experimental import pallas as pl
from jax.experimental.pallas import tpu as pltpu
from jax.sharding import Mesh
from jax.sharding import PartitionSpec as P

BF16 = jnp.bfloat16
F32 = jnp.float32
I32 = jnp.int32
I16 = jnp.int16
LANES = 128
UNROLL = 8
ROWS = 160


def shrink_steps(y, steps, *others):
    for step in steps:
        small = y < 8.0 * 2.0**-step
        y = y * jnp.where(small, 2.0**step, 1.0)
        others = tuple((v * jnp.where(small, 2.0 ** (step * way), 1.0), way) for v, way in others)
    return y, [v for v, _ in others]


def encode(c_ref, c32_ref, tab_ref):
    blocks = c_ref.shape[0]
    strings = tab_ref.shape[1]
    high = None
    for j in range(blocks):
        v = c_ref[j].astype(F32)
        c32_ref[j] = v
        m = jnp.maximum(jnp.abs(v[:strings]), jnp.abs(v[strings:]))
        high = m if high is None else jnp.maximum(high, m)
    high = jnp.broadcast_to(jnp.max(high, axis=(0, 1), keepdims=True), (strings, LANES))
    one = jnp.ones((strings, LANES), F32)
    _, (scale, back) = shrink_steps(high, (64, 32, 16, 8, 4, 2, 1), (one, 1), (one, -1))
    for j in range(blocks):
        re = c32_ref[j, pl.ds(0, strings, stride=2), :] * scale
        im = c32_ref[j, pl.ds(1, strings, stride=2), :] * scale
        size = jnp.maximum(jnp.abs(re), jnp.abs(im))
        power = jnp.zeros((strings, LANES), I32)
        for step in (16, 8, 4, 2, 1):
            small = size < 8.0 * 2.0**-step
            up = jnp.where(small, 2.0**step, 1.0)
            size, re, im = size * up, re * up, im * up
            power = power + jnp.where(small, step, 0)
        low = ((im * 512.0).astype(I32) & 8191) << 6 | power
        top = (re * 2.0**28).astype(I32)
        tab_ref[j] = ((top - low + (1 << 18)) >> 19) << 19 | low
    return back * 2.0**-28


def gather_block(tab_ref, idx_ref, sgn_ref, factor, p0, n):
    blocks, strings, _ = tab_ref.shape
    idx = idx_ref[pl.ds(p0, n), :]
    sign = sgn_ref[pl.ds(p0, n), :].astype(F32) * factor[:n]
    hi = lax.shift_right_logical(idx, 7)
    lo = idx & (LANES - 1)
    here = [hi == j for j in range(blocks)]
    values = []
    for a in range(0, strings, 2):
        got = [None, None]
        for j in range(blocks):
            for q in range(2):
                row = jnp.broadcast_to(tab_ref[j, a + q : a + q + 1, :], lo.shape)
                v = jnp.take_along_axis(row, lo, axis=1, mode="promise_in_bounds")
                got[q] = v if got[q] is None else jnp.where(here[j], v, got[q])
        for v in got:
            power = v & 31
            values.append(((v >> power).astype(F32) * sign, ((v << 13) >> power).astype(F32) * sign))
    return values


def gather_rows(tab_ref, idx_ref, sgn_ref, d_ref, factor, p0, n):
    parts = [gather_block(tab_ref, idx_ref, sgn_ref, factor, p0 + r, min(8, n - r)) for r in range(0, n, 8)]
    for a in range(tab_ref.shape[1]):
        for c in range(2):
            v = jnp.concatenate([part[a][c] for part in parts], axis=0) if len(parts) > 1 else parts[0][a][c]
            at = (a * 2 + c) * LANES
            d_ref[pl.ds(p0, n), at : at + LANES] = v.astype(BF16)


def slot_kernel(s_hbm, idx_hbm, sgn_hbm, first_hbm, m_ref, idx_ref, sgn_ref, s_ref, half_ref, sems):
    head, rest = pl.ds(0, UNROLL), pl.ds(UNROLL, s_ref.shape[0] - UNROLL)
    heads = pltpu.make_async_copy(s_hbm.at[head], s_ref.at[head], sems.at[3])
    others = pltpu.make_async_copy(s_hbm.at[rest], s_ref.at[rest], sems.at[4])
    fetches = [pltpu.make_async_copy(idx_hbm, idx_ref, sems.at[1]), pltpu.make_async_copy(sgn_hbm, sgn_ref, sems.at[2])]
    for fetch in [heads, others, *fetches]:
        fetch.start()
    width = m_ref.shape[2]
    rows = lax.broadcasted_iota(I32, (128, 128), 0).astype(I16)
    krow = lax.broadcasted_iota(I32, (width, 128), 0).astype(I16)
    one, zero = jnp.ones((width, 128), BF16), jnp.zeros((width, 128), BF16)

    def pair_of_blocks(d, out_ref, row):
        picks, pairs = [], []
        for e in range(2):
            code = s_ref[d + e, 0:1, :] * 16 + e * 8 + s_ref[d + e, 2:3, :]
            sign = jnp.broadcast_to(s_ref[d + e, 3:4, :].astype(F32), (128, 128)).astype(BF16)
            picks.append(jnp.where(rows == jnp.broadcast_to(code, (128, 128)).astype(I16), sign, zero[:128]))
            pair = jnp.broadcast_to(s_ref[d + e, 1:2, :], (16, 128)).astype(I16)
            pairs.append(jnp.where(krow == jnp.concatenate([pair] * (width // 16), axis=0), one, zero))
        m = lax.dot_general(
            jnp.concatenate(picks, axis=1),
            jnp.concatenate(pairs, axis=1),
            (((1,), (1,)), ((), ())),
            preferred_element_type=F32,
        ).astype(BF16)
        for a in range(8):
            out_ref[a, pl.ds(pl.multiple_of(row, 16), 16), :] = m[a * 16 : (a + 1) * 16, :]

    half = s_ref.shape[0] // 2

    def count(first, out_ref, begin, end):
        def body(i, carry):
            for d in range(0, UNROLL, 2):
                pair_of_blocks(first + i * UNROLL + d, out_ref, (i * UNROLL + d) * 8)
            return carry

        lax.fori_loop(begin, end, body, 0)

    heads.wait()
    count(0, half_ref, 0, 1)
    others.wait()
    count(0, half_ref, 1, half // UNROLL)
    send = pltpu.make_async_copy(half_ref, first_hbm, sems.at[0])
    send.start()
    count(half, m_ref, 0, half // UNROLL)
    send.wait()
    for fetch in fetches:
        fetch.wait()


def sigma_kernel(c_ref, idx_ref, sgn_ref, second_ref, v_hbm, first_hbm, o_ref, c32_ref, tab_ref, d_ref, e_ref, m_ref, v_ref, sems):
    half = second_ref.shape[1]
    fetches = [
        pltpu.make_async_copy(first_hbm, m_ref.at[:, :half, :], sems.at[0]),
        pltpu.make_async_copy(second_ref, m_ref.at[:, half:, :], sems.at[1]),
        pltpu.make_async_copy(v_hbm, v_ref, sems.at[2]),
    ]
    for fetch in fetches:
        fetch.start()
    pairs = v_ref.shape[0]
    strings = tab_ref.shape[1]
    factor = encode(c_ref, c32_ref, tab_ref)

    def body(i, carry):
        for r in range(0, ROWS, 16):
            p0 = pl.multiple_of(i * ROWS + r, 16)
            gather_rows(tab_ref, idx_ref, sgn_ref, d_ref, carry, p0, 16)
        return carry

    factor = lax.fori_loop(0, pairs // ROWS, body, factor)
    for p0 in range(pairs // ROWS * ROWS, pairs, 16):
        gather_rows(tab_ref, idx_ref, sgn_ref, d_ref, factor, p0, min(16, pairs - p0))
    for fetch in fetches:
        fetch.wait()
    width = 2 * LANES
    for h in range(0, strings, 2):
        at = slice(h * width, (h + 2) * width)
        e_ref[:, at] = jnp.dot(v_ref[...], d_ref[:, at], preferred_element_type=F32).astype(BF16)
    acc = None
    for a in range(strings):
        t = jnp.dot(m_ref[a, :, 0:pairs], e_ref[:, a * width : (a + 1) * width], preferred_element_type=F32)
        acc = t if acc is None else acc + t
    o_ref[...] = acc.astype(BF16)


def local(coeffs, integrals, beta_source, beta_sign, alpha_slots):
    strings, _, cols = coeffs.shape
    pairs = integrals.shape[0]
    blocks = alpha_slots.shape[1]
    vmem = pl.BlockSpec(memory_space=pltpu.VMEM)
    own = coeffs.reshape(strings * 2, cols)
    all_cols = lax.all_to_all(jnp.broadcast_to(own[None], (8, *own.shape)), ("x", "core"), 0, 0, tiled=True)
    def in_vmem(x):
        return pltpu.with_memory_space_constraint(x, pltpu.VMEM)

    def in_hbm(x):
        return pltpu.with_memory_space_constraint(x, pltpu.HBM)

    half = (strings, blocks * strings // 2, 512)
    hbm = pl.BlockSpec(memory_space=pltpu.HBM)
    first, second, source, sign = pl.pallas_call(
        slot_kernel,
        in_specs=[hbm, hbm, hbm],
        out_specs=[hbm, vmem, vmem, vmem],
        out_shape=[pltpu.HBM(half, BF16), pltpu.VMEM(half, BF16)] + [pltpu.VMEM((pairs, cols), I32)] * 2,
        scratch_shapes=[pltpu.VMEM(alpha_slots.shape[1:], I32), pltpu.VMEM(half, BF16), pltpu.SemaphoreType.DMA((5,))],
        compiler_params=pltpu.CompilerParams(vmem_limit_bytes=24 << 20),
        name="slot_counts",
    )(in_hbm(alpha_slots[0]), in_hbm(beta_source), in_hbm(beta_sign))
    parts = pl.pallas_call(
        sigma_kernel,
        in_specs=[vmem] * 4 + [hbm] * 2,
        out_specs=vmem,
        out_shape=jax.ShapeDtypeStruct((blocks * strings, 2 * cols), BF16),
        scratch_shapes=[
            pltpu.VMEM((8, 2 * strings, cols), F32),
            pltpu.VMEM((8, strings, cols), I32),
            pltpu.VMEM((pairs, 2 * strings * cols), BF16),
            pltpu.VMEM((pairs, 2 * strings * cols), BF16),
            pltpu.VMEM((strings, blocks * strings, 512), BF16),
            pltpu.VMEM((pairs, pairs), BF16),
            pltpu.SemaphoreType.DMA((3,)),
        ],
        compiler_params=pltpu.CompilerParams(vmem_limit_bytes=24 << 20),
        name="sigma_parts",
    )(in_vmem(all_cols), source, sign, second, in_hbm(integrals), in_hbm(first))
    pieces = lax.all_to_all(parts.reshape(4, 16, strings, 2 * cols), "y", 0, 0, tiled=True)
    half = jnp.sum(pieces.astype(F32), axis=0).astype(BF16)
    pieces = lax.all_to_all(half, "z", 0, 0, tiled=True)
    return jnp.sum(pieces.astype(F32), axis=0).reshape(strings, 2, cols)


def solution(mesh):
    fine = Mesh(mesh.devices.reshape(4, 16, 4, 2), ("y", "z", "x", "core"))
    a, b = ("y", "z"), ("x", "core")
    in_specs = (P(a, None, b), P(), P(None, b), P(None, b), P(a, None, None, None))
    return jax.shard_map(local, mesh=fine, in_specs=in_specs, out_specs=P(a, None, b), check_vma=False)
```

```python
import jax
import jax.numpy as jnp
from jax import lax
from jax.experimental import pallas as pl
from jax.experimental.pallas import tpu as pltpu
from jax.sharding import Mesh
from jax.sharding import PartitionSpec as P

BF16 = jnp.bfloat16
F32 = jnp.float32
I32 = jnp.int32
I16 = jnp.int16
LANES = 128
UNROLL = 16
ROWS = 240


def shrink_steps(y, steps, *others):
    for step in steps:
        small = y < 8.0 * 2.0**-step
        y = y * jnp.where(small, 2.0**step, 1.0)
        others = tuple((v * jnp.where(small, 2.0 ** (step * way), 1.0), way) for v, way in others)
    return y, [v for v, _ in others]


def encode(c_ref, c32_ref, tab_ref):
    blocks = c_ref.shape[0]
    strings = tab_ref.shape[1]
    high = None
    for j in range(blocks):
        v = c_ref[j].astype(F32)
        c32_ref[j] = v
        m = jnp.maximum(jnp.abs(v[:strings]), jnp.abs(v[strings:]))
        high = m if high is None else jnp.maximum(high, m)
    high = jnp.broadcast_to(jnp.max(high, axis=(0, 1), keepdims=True), (strings, LANES))
    one = jnp.ones((strings, LANES), F32)
    _, (scale, back) = shrink_steps(high, (64, 32, 16, 8, 4, 2, 1), (one, 1), (one, -1))
    for j in range(blocks):
        re = c32_ref[j, pl.ds(0, strings, stride=2), :] * scale
        im = c32_ref[j, pl.ds(1, strings, stride=2), :] * scale
        size = jnp.maximum(jnp.abs(re), jnp.abs(im))
        power = jnp.zeros((strings, LANES), I32)
        for step in (16, 8, 4, 2, 1):
            small = size < 8.0 * 2.0**-step
            up = jnp.where(small, 2.0**step, 1.0)
            size, re, im = size * up, re * up, im * up
            power = power + jnp.where(small, step, 0)
        low = ((im * 512.0).astype(I32) & 8191) << 6 | power
        top = (re * 2.0**28).astype(I32)
        tab_ref[j] = ((top - low + (1 << 18)) >> 19) << 19 | low
    return back * 2.0**-28


def gather_block(tab_ref, idx_ref, sgn_ref, factor, p0, n):
    blocks, strings, _ = tab_ref.shape
    idx = idx_ref[pl.ds(p0, n), :]
    sign = sgn_ref[pl.ds(p0, n), :].astype(F32) * factor[:n]
    hi = lax.shift_right_logical(idx, 7)
    lo = idx & (LANES - 1)
    here = [hi == j for j in range(blocks)]
    values = []
    for a in range(0, strings, 2):
        got = [None, None]
        for j in range(blocks):
            for q in range(2):
                row = jnp.broadcast_to(tab_ref[j, a + q : a + q + 1, :], lo.shape)
                v = jnp.take_along_axis(row, lo, axis=1, mode="promise_in_bounds")
                got[q] = v if got[q] is None else jnp.where(here[j], v, got[q])
        for v in got:
            power = v & 31
            values.append(((v >> power).astype(F32) * sign, ((v << 13) >> power).astype(F32) * sign))
    return values


def gather_rows(tab_ref, idx_ref, sgn_ref, d_ref, factor, p0, n):
    parts = [gather_block(tab_ref, idx_ref, sgn_ref, factor, p0 + r, min(8, n - r)) for r in range(0, n, 8)]
    for a in range(tab_ref.shape[1]):
        for c in range(2):
            v = jnp.concatenate([part[a][c] for part in parts], axis=0) if len(parts) > 1 else parts[0][a][c]
            at = (a * 2 + c) * LANES
            d_ref[pl.ds(p0, n), at : at + LANES] = v.astype(BF16)


def slot_kernel(s_hbm, idx_hbm, sgn_hbm, first_hbm, m_ref, idx_ref, sgn_ref, s_ref, half_ref, sems):
    head, rest = pl.ds(0, UNROLL), pl.ds(UNROLL, s_ref.shape[0] - UNROLL)
    heads = pltpu.make_async_copy(s_hbm.at[head], s_ref.at[head], sems.at[3])
    others = pltpu.make_async_copy(s_hbm.at[rest], s_ref.at[rest], sems.at[4])
    fetches = [pltpu.make_async_copy(idx_hbm, idx_ref, sems.at[1]), pltpu.make_async_copy(sgn_hbm, sgn_ref, sems.at[2])]
    for fetch in [heads, others, *fetches]:
        fetch.start()
    width = m_ref.shape[2]
    rows = lax.broadcasted_iota(I32, (128, 128), 0).astype(I16)
    krow = lax.broadcasted_iota(I32, (width, 128), 0).astype(I16)
    one, zero = jnp.ones((width, 128), BF16), jnp.zeros((width, 128), BF16)

    def pair_of_blocks(d, out_ref, row):
        picks, pairs = [], []
        for e in range(2):
            code = s_ref[d + e, 0:1, :] * 16 + e * 8 + s_ref[d + e, 2:3, :]
            sign = jnp.broadcast_to(s_ref[d + e, 3:4, :].astype(F32), (128, 128)).astype(BF16)
            picks.append(jnp.where(rows == jnp.broadcast_to(code, (128, 128)).astype(I16), sign, zero[:128]))
            pair = jnp.broadcast_to(s_ref[d + e, 1:2, :], (16, 128)).astype(I16)
            pairs.append(jnp.where(krow == jnp.concatenate([pair] * (width // 16), axis=0), one, zero))
        m = lax.dot_general(
            jnp.concatenate(picks, axis=1),
            jnp.concatenate(pairs, axis=1),
            (((1,), (1,)), ((), ())),
            preferred_element_type=F32,
        ).astype(BF16)
        for a in range(8):
            out_ref[a, pl.ds(pl.multiple_of(row, 16), 16), :] = m[a * 16 : (a + 1) * 16, :]

    half = s_ref.shape[0] // 2

    def count(first, out_ref, begin, end):
        def body(i, carry):
            for d in range(0, UNROLL, 2):
                pair_of_blocks(first + i * UNROLL + d, out_ref, (i * UNROLL + d) * 8)
            return carry

        lax.fori_loop(begin, end, body, 0)

    heads.wait()
    count(0, half_ref, 0, 1)
    others.wait()
    count(0, half_ref, 1, half // UNROLL)
    send = pltpu.make_async_copy(half_ref, first_hbm, sems.at[0])
    send.start()
    count(half, m_ref, 0, half // UNROLL)
    send.wait()
    for fetch in fetches:
        fetch.wait()


def sigma_kernel(c_ref, idx_ref, sgn_ref, second_ref, v_hbm, first_hbm, o_ref, c32_ref, tab_ref, d_ref, e_ref, m_ref, v_ref, sems):
    half = second_ref.shape[1]
    fetches = [
        pltpu.make_async_copy(first_hbm, m_ref.at[:, :half, :], sems.at[0]),
        pltpu.make_async_copy(second_ref, m_ref.at[:, half:, :], sems.at[1]),
        pltpu.make_async_copy(v_hbm, v_ref, sems.at[2]),
    ]
    for fetch in fetches:
        fetch.start()
    pairs = v_ref.shape[0]
    strings = tab_ref.shape[1]
    factor = encode(c_ref, c32_ref, tab_ref)

    def body(i, carry):
        for r in range(0, ROWS, 16):
            p0 = pl.multiple_of(i * ROWS + r, 16)
            gather_rows(tab_ref, idx_ref, sgn_ref, d_ref, carry, p0, 16)
        return carry

    factor = lax.fori_loop(0, pairs // ROWS, body, factor)
    for p0 in range(pairs // ROWS * ROWS, pairs, 16):
        gather_rows(tab_ref, idx_ref, sgn_ref, d_ref, factor, p0, min(16, pairs - p0))
    for fetch in fetches:
        fetch.wait()
    width = 2 * LANES
    for h in range(0, strings, 2):
        at = slice(h * width, (h + 2) * width)
        e_ref[:, at] = jnp.dot(v_ref[...], d_ref[:, at], preferred_element_type=F32).astype(BF16)
    acc = None
    for a in range(strings):
        t = jnp.dot(m_ref[a, :, 0:pairs], e_ref[:, a * width : (a + 1) * width], preferred_element_type=F32)
        acc = t if acc is None else acc + t
    o_ref[...] = acc.astype(BF16)


def local(coeffs, integrals, beta_source, beta_sign, alpha_slots):
    strings, _, cols = coeffs.shape
    pairs = integrals.shape[0]
    blocks = alpha_slots.shape[1]
    vmem = pl.BlockSpec(memory_space=pltpu.VMEM)
    own = coeffs.reshape(strings * 2, cols)
    all_cols = lax.all_to_all(jnp.broadcast_to(own[None], (8, *own.shape)), ("x", "core"), 0, 0, tiled=True)
    def in_vmem(x):
        return pltpu.with_memory_space_constraint(x, pltpu.VMEM)

    def in_hbm(x):
        return pltpu.with_memory_space_constraint(x, pltpu.HBM)

    half = (strings, blocks * strings // 2, 512)
    hbm = pl.BlockSpec(memory_space=pltpu.HBM)
    first, second, source, sign = pl.pallas_call(
        slot_kernel,
        in_specs=[hbm, hbm, hbm],
        out_specs=[hbm, vmem, vmem, vmem],
        out_shape=[pltpu.HBM(half, BF16), pltpu.VMEM(half, BF16)] + [pltpu.VMEM((pairs, cols), I32)] * 2,
        scratch_shapes=[pltpu.VMEM(alpha_slots.shape[1:], I32), pltpu.VMEM(half, BF16), pltpu.SemaphoreType.DMA((5,))],
        compiler_params=pltpu.CompilerParams(vmem_limit_bytes=24 << 20),
        name="slot_counts",
    )(in_hbm(alpha_slots[0]), in_hbm(beta_source), in_hbm(beta_sign))
    parts = pl.pallas_call(
        sigma_kernel,
        in_specs=[vmem] * 4 + [hbm] * 2,
        out_specs=vmem,
        out_shape=jax.ShapeDtypeStruct((blocks * strings, 2 * cols), BF16),
        scratch_shapes=[
            pltpu.VMEM((8, 2 * strings, cols), F32),
            pltpu.VMEM((8, strings, cols), I32),
            pltpu.VMEM((pairs, 2 * strings * cols), BF16),
            pltpu.VMEM((pairs, 2 * strings * cols), BF16),
            pltpu.VMEM((strings, blocks * strings, 512), BF16),
            pltpu.VMEM((pairs, pairs), BF16),
            pltpu.SemaphoreType.DMA((3,)),
        ],
        compiler_params=pltpu.CompilerParams(vmem_limit_bytes=24 << 20),
        name="sigma_parts",
    )(in_vmem(all_cols), source, sign, second, in_hbm(integrals), in_hbm(first))
    pieces = lax.all_to_all(parts.reshape(4, 16, strings, 2 * cols), "y", 0, 0, tiled=True)
    half = jnp.sum(pieces.astype(F32), axis=0).astype(BF16)
    pieces = lax.all_to_all(half, "z", 0, 0, tiled=True)
    return jnp.sum(pieces.astype(F32), axis=0).reshape(strings, 2, cols)


def solution(mesh):
    fine = Mesh(mesh.devices.reshape(4, 16, 4, 2), ("y", "z", "x", "core"))
    a, b = ("y", "z"), ("x", "core")
    in_specs = (P(a, None, b), P(), P(None, b), P(None, b), P(a, None, None, None))
    return jax.shard_map(local, mesh=fine, in_specs=in_specs, out_specs=P(a, None, b), check_vma=False)
```
